32 devices in a mesh: row: 4 (over x, core), grp: 8 (over z, y).
Axes of the slice: x: 2, y: 2, z: 4, core: 2. Of those that a mesh axis runs over, the one named last changes fastest.
Arguments:
- integrals: bfloat16 [32, 512, 256], P('grp', 'row'), may hold values from -1.1953125 to 1.1953125
- amplitudes: bfloat16 [32, 1024, 256], P('grp', 'row'), may hold values from -1.796875 to 1.796875
- pair_orbs: int32 [32, 8], P('grp', 'row'), may hold values from 0 to 3, as said below
- pair_count: int32 [8, 4], P('grp', 'row'), may hold values from 1 to 4, as said below
- neighbours: int32 [32, 16], P('grp', 'row'), may hold values from 0 to 11
- coupling: float32 [32, 16], P('grp', 'row'), may hold values from -1.8 to 1.8
- bases: bfloat16 [32, 1024, 256], P('grp', 'row'), may hold values from -0.375 to 0.375
- virt_energy: float32 [32, 1024], P('grp', 'row'), may hold values from 0.3 to 3
- occ_energy: float32 [32, 4], P('grp', 'row'), may hold values from -1.5 to -0.3
Outputs:
- residual: float32 [32, 1024, 256], P('grp', 'row')
The draws below stay inside these ranges and needn't reach their ends.
Inputs may be any that keep to these rules, and one draw needn't show every extreme that they name: `pair_orbs`: in the columns of row r the first orbital of every pair is orbital r of the group, the one owned by that device; the second is any orbital of the group. `pair_count`: live slots come first on each device; some device holds 4 live pairs in every draw.
All inputs are finite; a program needn't handle non-finite values.
Results may differ from the reference program's by a relative error of at most 0.0007.
Values may be sent and summed in bfloat16 or wider, within the bound.
No kernel may reach another device: no remote copies, remote signals or barrier semaphores. Data moves between devices by JAX's collectives and lax.ppermute only.
A program may use at most 64 MiB of HBM per device.

```python
import math
import jax
import jax.numpy as jnp
from jax import lax

VIRT = 256
AUX = 512
ORB_DEV = 1
PAIRS_DEV = 4
NEIGH = 4
GROUP_ORBS = 4
NOCC = 32
N_ROW = 4
N_GRP = 8


def counts_table(key):
    base = jax.random.randint(jax.random.fold_in(key, 11), (N_GRP, N_ROW), 1, PAIRS_DEV // 2 + 1)
    busy = jax.random.randint(jax.random.fold_in(key, 12), (N_GRP, N_ROW), 0, 8) == 0
    table = jnp.where(busy, PAIRS_DEV, base)
    first = jax.random.randint(jax.random.fold_in(key, 13), (), 0, N_GRP)
    second = jax.random.randint(jax.random.fold_in(key, 14), (), 0, N_ROW)
    return table.at[first, second].set(PAIRS_DEV).astype(jnp.int32)


def draw_pair_count(key, part):
    return counts_table(key)


def draw_pair_orbs(key, part):
    shape = (N_GRP, PAIRS_DEV, N_ROW)
    offset = jax.random.randint(jax.random.fold_in(key, 21), shape, 0, ORB_DEV)
    owned = jnp.arange(N_ROW, dtype=jnp.int32)[None, None, :] * ORB_DEV + offset
    other = jax.random.randint(jax.random.fold_in(key, 22), shape, 0, GROUP_ORBS)
    stacked = jnp.stack([owned, other], axis=-1)
    return stacked.reshape(N_GRP * PAIRS_DEV, N_ROW * 2).astype(jnp.int32)


def place_ends(values, stream_key, least, top_value):
    place = [jax.random.randint(jax.random.fold_in(stream_key, axis), (), 0, length) for axis, length in enumerate(values.shape)]
    widest = values.shape.index(max(values.shape))
    neighbour = place[:widest] + [(place[widest] + 1) % values.shape[widest]] + place[widest + 1:]
    return values.at[tuple(place)].set(least).at[tuple(neighbour)].set(top_value)


def shard_levels(key, shape, cuts, least, largest):
    def one(dim, blocks):
        steps = jax.random.uniform(jax.random.fold_in(jax.random.fold_in(key, 6), dim), (blocks,), jnp.float32, least / len(cuts), largest / len(cuts))
        return jnp.repeat(jnp.exp(steps), shape[dim] // blocks).reshape((-1,) + (1,) * (len(shape) - dim - 1))

    gain = one(*cuts[0])
    for cut in cuts[1:]:
        gain = gain * one(*cut)
    return gain


def centred(stream_key, extent, deviation, most, cuts=(), held_as=jnp.bfloat16):
    drawn = deviation * jax.random.normal(stream_key, extent, jnp.float32)
    if cuts:
        drawn = drawn * shard_levels(stream_key, extent, cuts, -0.22, 0.18)
    return jnp.clip(drawn, -most, most).astype(held_as)


def setup_inputs(seed: int = 0) -> dict:
    seeds = jax.random.split(jax.random.key(seed), 10)
    integrals = centred(seeds[0], (NOCC, AUX, VIRT), 0.2, 1.1953125, ((0, 8), (1, 4)))
    amplitudes = centred(seeds[1], (PAIRS_DEV * N_GRP, N_ROW * VIRT, VIRT), 0.3, 1.796875, ((0, 8), (1, 4)))
    pair_orbs = draw_pair_orbs(jax.random.fold_in(seeds[9], 71), 0)
    pair_count = draw_pair_count(jax.random.fold_in(seeds[9], 71), 0)
    neighbours = place_ends(jax.random.randint(seeds[4], (PAIRS_DEV * N_GRP, NEIGH * N_ROW), 0, 3 * PAIRS_DEV), jax.random.fold_in(seeds[4], 1), 0, (3 * PAIRS_DEV) - 1).astype(jnp.int32)
    coupling = centred(seeds[5], (PAIRS_DEV * N_GRP, NEIGH * N_ROW), 0.3, 1.8, ((0, 8), (1, 4)), jnp.float32)
    bases = centred(seeds[6], (PAIRS_DEV * N_GRP, N_ROW * VIRT, VIRT), VIRT ** -0.5, 0.375, ((0, 8), (1, 4)))
    virt_energy = jnp.clip(jnp.exp(math.log(3.0) - 2.3025851 * jax.random.uniform(seeds[7], (PAIRS_DEV * N_GRP, N_ROW * VIRT), jnp.float32) ** shard_levels(seeds[7], (PAIRS_DEV * N_GRP, N_ROW * VIRT), ((0, 8), (1, 4)), -0.2, 0.2)), 0.3, 3.0)
    occ_energy = jnp.clip(-1.5 + 1.2 * jax.random.uniform(seeds[8], (PAIRS_DEV * N_GRP, N_ROW), jnp.float32) ** shard_levels(seeds[8], (PAIRS_DEV * N_GRP, N_ROW), ((0, 8), (1, 4)), -0.2, 0.2), -1.5, -0.3)
    return {"integrals": integrals, "amplitudes": amplitudes, "pair_orbs": pair_orbs, "pair_count": pair_count, "neighbours": neighbours, "coupling": coupling, "bases": bases, "virt_energy": virt_energy, "occ_energy": occ_energy}


def per_slot(array, tail):
    shaped = array.reshape((N_GRP, PAIRS_DEV, N_ROW) + tail)
    return jnp.swapaxes(shaped, 1, 2)


def reference(integrals, amplitudes, pair_orbs, pair_count, neighbours, coupling, bases, virt_energy, occ_energy):
    width = PAIRS_DEV
    groups = integrals.reshape(N_GRP, GROUP_ORBS, AUX, VIRT)
    amps = per_slot(amplitudes, (VIRT, VIRT))
    live = jnp.arange(width, dtype=jnp.int32)[None, None, :] < pair_count[:, :, None]
    amps = jnp.where(live[..., None, None], amps, jnp.zeros((), jnp.bfloat16))
    basis = per_slot(bases, (VIRT, VIRT))
    orbs = per_slot(pair_orbs, (2,))
    lists = per_slot(neighbours, (NEIGH,))
    weights_in = per_slot(coupling, (NEIGH,))
    venergy = per_slot(virt_energy, (VIRT,))
    oenergy = per_slot(occ_energy, ())

    def transform(item):
        base_g, amp_g = item
        first = jnp.einsum('rpac,rpcd->rpad', base_g.astype(jnp.float32), amp_g.astype(jnp.float32)).astype(jnp.bfloat16)
        return jnp.einsum('rpad,rpbd->rpab', first.astype(jnp.float32), base_g.astype(jnp.float32)).astype(jnp.bfloat16)

    moved = lax.map(transform, (basis, amps))
    zero = jnp.zeros((1, N_ROW, width, VIRT, VIRT), jnp.bfloat16)
    padded = jnp.concatenate([zero, moved, zero], axis=0)

    def per_group(g):
        ints = groups[g]
        orb = orbs[g]
        left = ints[orb[..., 0]].astype(jnp.float32)
        right = ints[orb[..., 1]].astype(jnp.float32)
        integ = jnp.einsum('rpxa,rpxb->rpab', left, right)
        window = lax.dynamic_slice_in_dim(padded, g, 3, 0)
        window = jnp.swapaxes(window, 0, 1).reshape(N_ROW, 3 * width, VIRT, VIRT)
        onehot = (lists[g][..., None] == jnp.arange(3 * width, dtype=jnp.int32)).astype(jnp.float32)
        weights = jnp.sum(weights_in[g][..., None] * onehot, axis=2)
        combined = jnp.einsum('rpm,rmab->rpab', weights, window.astype(jnp.float32)).astype(jnp.bfloat16)
        base_g = basis[g].astype(jnp.float32)
        back_first = jnp.einsum('rpca,rpcb->rpab', base_g, combined.astype(jnp.float32)).astype(jnp.bfloat16)
        back = jnp.einsum('rpac,rpcb->rpab', back_first.astype(jnp.float32), base_g)
        energy = venergy[g]
        denom = energy[..., :, None] + energy[..., None, :] - oenergy[g][..., None, None]
        resid = integ + denom * amps[g].astype(jnp.float32) - back
        return jnp.where(live[g][..., None, None], resid, jnp.zeros((), jnp.float32))

    result = lax.map(per_group, jnp.arange(N_GRP, dtype=jnp.int32))
    return jnp.swapaxes(result, 1, 2).reshape(N_GRP * width, N_ROW * VIRT, VIRT)
```

```python
import jax
import jax.numpy as jnp
from jax import lax
from jax.sharding import PartitionSpec as P

CHUNKS = 2


def row_gather(array, dim):
    count = lax.axis_size("row")
    if count & (count - 1):
        return lax.all_gather(array, "row", axis=dim, tiled=True)
    step = count // 2
    while step:
        pairs = [(i, i ^ step) for i in range(count)]
        array = jnp.concatenate([array, lax.ppermute(array, "row", pairs)], axis=dim)
        step //= 2
    return array


def exchange(moved):
    count = lax.axis_size("grp")
    if count % 2:
        up = [(i, i + 1) for i in range(count - 1)]
        down = [(j, i) for i, j in up]
        return lax.ppermute(moved, "grp", down), lax.ppermute(moved, "grp", up)
    swap = [(i, i ^ 1) for i in range(count)]
    ahead = [(i, i + 2) for i in range(0, count - 2, 2)] + [(i, i - 2) for i in range(3, count, 2)]
    near = lax.ppermute(moved, "grp", swap)
    far = lax.ppermute(near, "grp", ahead)
    return near, far


def local(
    integrals,
    amplitudes,
    pair_orbs,
    pair_count,
    neighbours,
    coupling,
    bases,
    virt_energy,
    occ_energy,
):
    width = amplitudes.shape[0]
    live = jnp.arange(width, dtype=jnp.int32) < pair_count[0, 0]
    amps = jnp.where(live[:, None, None], amplitudes, jnp.zeros((), jnp.bfloat16))
    first_orb = pair_orbs[:, 0]
    second_orb = pair_orbs[:, 1]
    piece = row_gather(integrals, 1)
    left = jnp.take(piece, first_orb, axis=0)
    right = jnp.take(piece, second_orb, axis=0)
    integ = jnp.einsum("pxa,pxb->pab", left, right, preferred_element_type=jnp.float32)
    first = jnp.einsum("pac,pcd->pad", bases, amps, preferred_element_type=jnp.float32).astype(
        jnp.bfloat16
    )
    moved = jnp.einsum("pad,pbd->pab", first, bases, preferred_element_type=jnp.float32).astype(
        jnp.bfloat16
    )
    size = width // CHUNKS if width % CHUNKS == 0 else width
    near, far = [], []
    for start in range(0, width, size):
        got, passed = exchange(moved[start : start + size])
        near.append(got)
        far.append(passed)
    window = jnp.concatenate(near + [moved] + far, axis=0)
    even = lax.axis_index("grp") % 2 == 0
    if lax.axis_size("grp") % 2:
        even = jnp.bool_(True)
    block = neighbours // width
    place = jnp.where(even, 2 - block, block) * width + neighbours % width
    onehot = (place[:, :, None] == jnp.arange(3 * width, dtype=jnp.int32)).astype(jnp.float32)
    weights = jnp.sum(coupling[:, :, None] * onehot, axis=1)
    combined = jnp.einsum(
        "pm,mab->pab", weights, window.astype(jnp.float32), precision=lax.Precision.HIGHEST
    ).astype(jnp.bfloat16)
    back_first = jnp.einsum(
        "pca,pcb->pab", bases, combined, preferred_element_type=jnp.float32
    ).astype(jnp.bfloat16)
    back = jnp.einsum("pac,pcb->pab", back_first, bases, preferred_element_type=jnp.float32)
    denom = virt_energy[:, :, None] + virt_energy[:, None, :] - occ_energy[:, :, None]
    resid = integ + denom * amps.astype(jnp.float32) - back
    return jnp.where(live[:, None, None], resid, jnp.zeros((), jnp.float32))


def solution(mesh):
    placed = (
        P("grp", "row", None),
        P("grp", "row", None),
        P("grp", "row"),
        P("grp", "row"),
        P("grp", "row"),
        P("grp", "row"),
        P("grp", "row", None),
        P("grp", "row"),
        P("grp", "row"),
    )
    return jax.shard_map(
        local, mesh=mesh, in_specs=placed, out_specs=P("grp", "row", None), check_vma=False
    )
```

```python
import functools

import jax
import jax.numpy as jnp
from jax import lax
from jax.experimental import pallas as pl
from jax.experimental.pallas import tpu as pltpu
from jax.sharding import PartitionSpec as P


BF16 = jnp.bfloat16
F32 = jnp.float32
VMEM = pltpu.VMEM
SMEM = pltpu.SMEM
HBM = pltpu.HBM
GRANT = 8 << 20


def dot(a, b, dims):
    return lax.dot_general(a, b, (dims, ((), ())), preferred_element_type=F32)


def call(kernel, outs, inputs, flops, scratch=(), aliases=()):
    values, specs = [], []
    for space, value in inputs:
        if space in (VMEM, HBM):
            value = pltpu.with_memory_space_constraint(value, space)
        values.append(value)
        specs.append(pl.BlockSpec(memory_space=space))
    shapes, out_specs = [], []
    for space, shape, dtype in outs:
        plain = space is pl.ANY
        shapes.append(jax.ShapeDtypeStruct(shape, dtype) if plain else space(shape, dtype))
        out_specs.append(pl.BlockSpec(memory_space=space))
    size = sum(value.size * value.dtype.itemsize for value in values)
    return pl.pallas_call(
        kernel,
        out_shape=shapes,
        in_specs=specs,
        out_specs=out_specs,
        scratch_shapes=scratch,
        input_output_aliases=dict(aliases),
        cost_estimate=pl.CostEstimate(flops=flops, bytes_accessed=16 * size, transcendentals=0),
        compiler_params=pltpu.CompilerParams(vmem_limit_bytes=GRANT),
    )(*values)


def transform(base, amp):
    first = dot(base, amp, ((1,), (0,))).astype(BF16)
    return dot(first, base, ((1,), (1,))).astype(BF16)


def lead_kernel(count, amps, bases, *refs):
    small = (len(refs) - 6) // 2
    sources, (out, amps_out, bases_out, count_out) = refs[:small], refs[small : small + 4]
    targets, (number, sems) = refs[small + 4 : -2], refs[-2:]
    width = amps.shape[0]
    first = pltpu.make_async_copy(count, number, sems.at[2, 0])
    loads = [
        [
            pltpu.make_async_copy(bases.at[slot], bases_out.at[slot], sems.at[0, slot]),
            pltpu.make_async_copy(amps.at[slot], amps_out.at[slot], sems.at[1, slot]),
        ]
        for slot in range(width)
    ]
    others = [
        pltpu.make_async_copy(source, target, sems.at[3, n])
        for n, (source, target) in enumerate(zip(sources, targets))
    ]
    for load in loads[0] + [first] + sum(loads[1:], []) + others:
        load.start()
    for load in loads[0]:
        load.wait()
    out[...] = transform(bases_out[0], amps_out[0])
    first.wait()
    count_out[...] = jnp.full(count_out.shape, number[0, 0], jnp.int32)
    for load in sum(loads[1:], []) + others:
        load.wait()


def rest_kernel(count, amps, bases, *outs):
    for slot, out in enumerate(outs, 1):
        live = jnp.where(slot < count[...], jnp.float32(1), jnp.float32(0)).astype(BF16)
        out[...] = transform(bases[slot], amps[slot] * live)


def integ_kernel(orbs, occ, energy, amps, *refs):
    pieces, (out, held, sems) = refs[:-3], refs[-3:]
    width = amps.shape[0]
    column = energy[...].T
    left = jnp.concatenate([piece[orbs[0, 0]] for piece in pieces], axis=0).T
    stores = []
    for slot in range(width):
        right = jnp.concatenate([piece[orbs[1, slot]] for piece in pieces], axis=0)
        denom = column[:, slot : slot + 1] + energy[slot : slot + 1, :] - occ[0, slot]
        integ = dot(left, right, ((1,), (0,)))
        held[slot] = integ + denom * amps[slot].astype(F32)
        stores.append(pltpu.make_async_copy(held.at[slot], out.at[slot], sems.at[slot]))
        stores[slot].start()
    for store in stores:
        store.wait()


def add_tiles(rows, columns, weights, tiles, out, before=None):
    width, height = out.shape[0], out.shape[1]
    total = weights.shape[0] // width

    def step(block, carry):
        at = pl.ds(pl.multiple_of(block * rows, rows), rows)
        values = [tile[at, :].astype(F32) for tile in tiles]
        for slot in range(width):
            acc = None if before is None else before[slot, at, :]
            for m, value in zip(columns, values):
                row = slot * total + m
                term = weights[row : row + 1, :] * value
                acc = term if acc is None else acc + term
            out[slot, at, :] = acc
        return carry

    lax.fori_loop(0, height // rows, step, 0)


def gather_kernel(columns, weights, *refs):
    add_tiles(16, columns, weights, refs[:-1], refs[-1])


def final_kernel(columns, count, weights, base, bases, sums, *refs):
    tiles, (out, held, sems) = refs[:-3], refs[-3:]
    width = base.shape[0]
    half = width // 2
    total = weights.shape[0] // width
    loads = [pltpu.make_async_copy(base.at[s], held.at[s], sems.at[0, s]) for s in range(width)]
    stores = [pltpu.make_async_copy(held.at[s], out.at[s], sems.at[1, s]) for s in range(width)]
    for load in loads:
        load.start()
    number = jnp.max(count[...])

    def some(slots):
        combined = []
        for slot in slots:
            acc = sums[slot]
            for m, tile in zip(columns, tiles):
                row = slot * total + m
                acc = acc + weights[row : row + 1, :] * tile[...].astype(F32)
            combined.append(acc.astype(BF16))
        firsts = [dot(bases[s], c, ((0,), (0,))).astype(BF16) for s, c in zip(slots, combined)]
        for slot, first in zip(slots, firsts):
            back = dot(first, bases[slot], ((1,), (0,)))
            live = jnp.broadcast_to(slot < count[...], back.shape)
            loads[slot].wait()
            held[slot] = jnp.where(live, held[slot] - back, jnp.float32(0))
            stores[slot].start()

    some(range(half))

    @pl.when(number > half)
    def _():
        some(range(half, width))

    @pl.when(number <= half)
    def _():
        for slot in range(half, width):
            loads[slot].wait()
            held[slot] = jnp.zeros(held.shape[1:], F32)
            stores[slot].start()

    for store in stores:
        store.wait()


def row_pieces(array):
    count = lax.axis_size("row")
    pieces = [array]
    if count & (count - 1):
        for shift in range(1, count):
            pairs = [(i, (i + shift) % count) for i in range(count)]
            pieces.append(lax.ppermute(array, "row", pairs))
        return pieces
    step = count // 2
    while step:
        pairs = [(i, i ^ step) for i in range(count)]
        pieces += [lax.ppermute(piece, "row", pairs) for piece in pieces]
        step //= 2
    return pieces


def tile_weights(neighbours, coupling, width, virt):
    levels = lax.axis_size("grp") // 2
    group = lax.axis_index("grp")
    level = lax.shift_right_logical(group, 1)
    even = (group & 1) == 0
    odd_level = (level & 1) == 1
    inside = jnp.where(even, level > 0, level < levels - 1)
    tail = jnp.where(odd_level == even, 3 * width - 1, 3 * width)
    block = (neighbours >= width).astype(jnp.int32) + (neighbours >= 2 * width).astype(jnp.int32)
    kind = jnp.where(even, 2 - block, block)
    scale = jnp.where((kind < 2) | inside, coupling, 0.0)
    place = neighbours + (kind - block) * width
    place = jnp.where(place == 3 * width - 1, tail, place)
    total = 3 * width + 1
    shape = (width, total, virt, neighbours.shape[1])
    index = lax.broadcasted_iota(jnp.int32, shape, 1)
    hit = place[:, None, None, :] == index
    table = jnp.sum(jnp.where(hit, scale[:, None, None, :], 0.0), axis=3)
    return table.reshape(width * total, virt)


def level_pairs(count, phase):
    half = count // 2
    other = []
    for z in range(half):
        mate = z ^ 1 if phase == 0 else (z + 1 if z % 2 else z - 1)
        other.append(mate if 0 <= mate < half else z)
    return [(2 * z + y, 2 * other[z] + y) for z in range(half) for y in range(2)]


def local(
    integrals,
    amplitudes,
    pair_orbs,
    pair_count,
    neighbours,
    coupling,
    bases,
    virt_energy,
    occ_energy,
):
    width, virt = amplitudes.shape[0], amplitudes.shape[1]
    count = lax.axis_size("grp")
    cube = 2 * virt * virt * virt
    tile = (VMEM, (virt, virt), BF16)
    stack = (VMEM, (width, virt, virt), BF16)
    wide = (VMEM, (width, virt, virt), F32)
    last = width - 1
    dma = pltpu.SemaphoreType.DMA

    small = (neighbours, coupling, virt_energy, pair_orbs.T, occ_energy.T)
    own, amps, basis, counts, *small = call(
        lead_kernel,
        [tile, stack, stack, (VMEM, (1, virt), jnp.int32)]
        + [(VMEM, value.shape, value.dtype) for value in small],
        [(pl.ANY, pair_count), (HBM, amplitudes), (HBM, bases)] + [(HBM, value) for value in small],
        2 * cube, [SMEM((1, 1), jnp.int32), dma((4, max(width, len(small))))],
    )
    neighbours, coupling, virt_energy, orbs, occ = small
    own = [own] + list(call(
        rest_kernel, [tile] * last, [(VMEM, counts), (VMEM, amps), (VMEM, basis)],
        2 * last * cube,
    ))
    weights = tile_weights(neighbours, coupling, width, virt)

    swap = [(i, i ^ 1) for i in range(count)]
    ring = [(i, (i + 2) % count if i % 2 == 0 else (i - 2) % count) for i in range(count)]
    near = [lax.ppermute(t, "grp", swap) for t in own]
    far = [lax.ppermute(near[n], "grp", ring) for n in range(last)]
    far_a = lax.ppermute(near[last], "grp", level_pairs(count, 0))
    far_b = lax.ppermute(near[last], "grp", level_pairs(count, 1))

    pieces = row_pieces(integrals)
    aux = sum(piece.shape[1] for piece in pieces)
    base = call(
        integ_kernel, [(HBM, (width, virt, virt), F32)],
        [(SMEM, orbs), (SMEM, occ), (VMEM, virt_energy), (VMEM, amplitudes)]
        + [(VMEM, piece) for piece in pieces], 2 * width * virt * virt * aux,
        [VMEM((width, virt, virt), F32), dma((width,))],
    )[0]
    sums = call(
        functools.partial(gather_kernel, range(3 * width - 1)), [wide],
        [(VMEM, weights)] + [(VMEM, t) for t in near + own + far], 8 * width * virt * virt,
    )[0]
    return call(
        functools.partial(final_kernel, (3 * width - 1, 3 * width)),
        [(pl.ANY, (width, virt, virt), F32)],
        [(VMEM, counts), (VMEM, weights), (HBM, base), (VMEM, bases), (VMEM, sums),
         (VMEM, far_a), (VMEM, far_b)],
        2 * width * cube, [VMEM((width, virt, virt), F32), dma((2, width))],
    )[0]


def solution(mesh):
    placed = (
        P("grp", "row", None),
        P("grp", "row", None),
        P("grp", "row"),
        P("grp", "row"),
        P("grp", "row"),
        P("grp", "row"),
        P("grp", "row", None),
        P("grp", "row"),
        P("grp", "row"),
    )

    return jax.shard_map(
        local, mesh=mesh, in_specs=placed, out_specs=P("grp", "row", None), check_vma=False
    )
```

```python
import functools

import jax
import jax.numpy as jnp
from jax import lax
from jax.experimental import pallas as pl
from jax.experimental.pallas import tpu as pltpu
from jax.sharding import PartitionSpec as P


BF16 = jnp.bfloat16
F32 = jnp.float32
VMEM = pltpu.VMEM
SMEM = pltpu.SMEM
HBM = pltpu.HBM
GRANT = 8 << 20


def dot(a, b, dims):
    return lax.dot_general(a, b, (dims, ((), ())), preferred_element_type=F32)


def call(kernel, outs, inputs, flops, scratch=(), aliases=()):
    values, specs = [], []
    for space, value in inputs:
        if space in (VMEM, HBM):
            value = pltpu.with_memory_space_constraint(value, space)
        values.append(value)
        specs.append(pl.BlockSpec(memory_space=space))
    shapes, out_specs = [], []
    for space, shape, dtype in outs:
        plain = space is pl.ANY
        shapes.append(jax.ShapeDtypeStruct(shape, dtype) if plain else space(shape, dtype))
        out_specs.append(pl.BlockSpec(memory_space=space))
    size = sum(value.size * value.dtype.itemsize for value in values)
    return pl.pallas_call(
        kernel,
        out_shape=shapes,
        in_specs=specs,
        out_specs=out_specs,
        scratch_shapes=scratch,
        input_output_aliases=dict(aliases),
        cost_estimate=pl.CostEstimate(flops=flops, bytes_accessed=16 * size, transcendentals=0),
        compiler_params=pltpu.CompilerParams(vmem_limit_bytes=GRANT),
    )(*values)


def transform(base, amp):
    first = dot(base, amp, ((1,), (0,))).astype(BF16)
    return dot(first, base, ((1,), (1,))).astype(BF16)


def lead_kernel(amps, bases, *refs):
    small = (len(refs) - 4) // 2
    sources, (out, amps_out, bases_out) = refs[:small], refs[small : small + 3]
    targets, sems = refs[small + 3 : -1], refs[-1]
    width = amps.shape[0]
    loads = [
        [
            pltpu.make_async_copy(bases.at[slot], bases_out.at[slot], sems.at[0, slot]),
            pltpu.make_async_copy(amps.at[slot], amps_out.at[slot], sems.at[1, slot]),
        ]
        for slot in range(width)
    ]
    others = [
        pltpu.make_async_copy(source, target, sems.at[2, n])
        for n, (source, target) in enumerate(zip(sources, targets))
    ]
    for load in sum(loads, []) + others:
        load.start()
    for load in loads[0]:
        load.wait()
    out[...] = transform(bases_out[0], amps_out[0])
    for load in sum(loads[1:], []) + others:
        load.wait()


def rest_kernel(count, amps, bases, *outs):
    for slot, out in enumerate(outs, 1):
        amp = jnp.where(slot < count[0, 0], amps[slot], jnp.zeros((), BF16))
        out[...] = transform(bases[slot], amp)


def mark_kernel(source, out):
    out[...] = source[...]


def in_halves(count, width, work):
    half = width // 2
    work(range(half))

    @pl.when(count[0, 0] > half)
    def _():
        work(range(half, width))


def integ_kernel(orbs, occ, count, energy, amps, *refs):
    pieces, (out, held, sems) = refs[:-3], refs[-3:]
    width = amps.shape[0]
    loads = [pltpu.make_async_copy(amps.at[s], held.at[s], sems.at[s]) for s in range(width)]
    for load in loads:
        load.start()
    column = energy[...].T
    left = [piece[orbs[0, 0]].T for piece in pieces]

    def products(slots):
        for slot in slots:
            terms = [dot(a, b[orbs[1, slot]], ((1,), (0,))) for a, b in zip(left, pieces)]
            out[slot] = sum(terms[1:], terms[0])

    def energies(slots):
        for slot in slots:
            denom = column[:, slot : slot + 1] + energy[slot : slot + 1, :] - occ[0, slot]
            out[slot] += denom * held[slot].astype(F32)

    in_halves(count, width, products)
    for load in loads:
        load.wait()
    in_halves(count, width, energies)


def add_tiles(rows, columns, weights, tiles, out, slots, before):
    total = weights.shape[0] // out.shape[0]

    def step(block, carry):
        at = pl.ds(pl.multiple_of(block * rows, rows), rows)
        values = [tile[at, :].astype(F32) for tile in tiles]
        for slot in slots:
            acc = out[slot, at, :] if before else None
            for m, value in zip(columns, values):
                row = slot * total + m
                term = weights[row : row + 1, :] * value
                acc = term if acc is None else acc + term
            out[slot, at, :] = acc
        return carry

    lax.fori_loop(0, out.shape[1] // rows, step, 0)


def gather_kernel(columns, count, weights, *refs):
    tiles, (out, held, sems) = refs[:-3], refs[-3:]
    width = out.shape[0]
    own, tiles = tiles[:width], tiles[width:]
    loads = [pltpu.make_async_copy(own[s], held.at[s], sems.at[s]) for s in range(width)]
    for load in loads:
        load.start()
    in_halves(count, width, lambda slots: add_tiles(16, columns, weights, tiles, out, slots, False))
    for load in loads:
        load.wait()
    own = [held.at[s] for s in range(width)]
    place = range(width, 2 * width)
    in_halves(count, width, lambda slots: add_tiles(16, place, weights, own, out, slots, True))


def final_kernel(columns, count, token, weights, base, bases, sums, *refs):
    tiles, (out, held, sems) = refs[:-3], refs[-3:]
    width = base.shape[0]
    half = width // 2
    total = weights.shape[0] // width
    stores = [pltpu.make_async_copy(held.at[s], out.at[s], sems.at[s]) for s in range(width)]

    @pl.when(count[0, 0] <= half)
    def _():
        for slot in range(half, width):
            held[slot] = jnp.zeros(held.shape[1:], F32)
            stores[slot].start()

    def some(slots):
        combined = []
        for slot in slots:
            acc = sums[slot]
            for m, tile in zip(columns, tiles):
                row = slot * total + m
                acc = acc + weights[row : row + 1, :] * tile[...].astype(F32)
            combined.append(acc.astype(BF16))
        firsts = [dot(bases[s], c, ((0,), (0,))).astype(BF16) for s, c in zip(slots, combined)]
        for slot, first in zip(slots, firsts):
            back = dot(first, bases[slot], ((1,), (0,)))
            value = base[slot] - back
            held[slot] = jnp.where(slot < count[0, 0], value, jnp.float32(0))
            stores[slot].start()

    in_halves(count, width, some)
    for store in stores:
        store.wait()


def row_pieces(array):
    count = lax.axis_size("row")
    pieces = [array]
    if count & (count - 1):
        for shift in range(1, count):
            pairs = [(i, (i + shift) % count) for i in range(count)]
            pieces.append(lax.ppermute(array, "row", pairs))
        return pieces
    step = count // 2
    while step:
        pairs = [(i, i ^ step) for i in range(count)]
        piece = jnp.concatenate(pieces, axis=1)
        pieces = [piece, lax.ppermute(piece, "row", pairs)]
        step //= 2
    return pieces


def tile_weights(neighbours, coupling, width, virt):
    levels = lax.axis_size("grp") // 2
    group = lax.axis_index("grp")
    level = lax.shift_right_logical(group, 1)
    even = (group & 1) == 0
    inside = jnp.where(even, level > 0, level < levels - 1)
    block = (neighbours >= width).astype(jnp.int32) + (neighbours >= 2 * width).astype(jnp.int32)
    kind = jnp.where(even, 2 - block, block)
    scale = jnp.where((kind < 2) | inside, coupling, 0.0)
    place = neighbours + (kind - block) * width
    shape = (width, 3 * width, virt, neighbours.shape[1])
    index = lax.broadcasted_iota(jnp.int32, shape, 1)
    hit = place[:, None, None, :] == index
    table = jnp.sum(jnp.where(hit, scale[:, None, None, :], 0.0), axis=3)
    return table.reshape(width * 3 * width, virt)


def local(
    integrals,
    amplitudes,
    pair_orbs,
    pair_count,
    neighbours,
    coupling,
    bases,
    virt_energy,
    occ_energy,
):
    width, virt = amplitudes.shape[0], amplitudes.shape[1]
    count = lax.axis_size("grp")
    cube = 2 * virt * virt * virt
    tile = (VMEM, (virt, virt), BF16)
    stack = (VMEM, (width, virt, virt), BF16)
    wide = (VMEM, (width, virt, virt), F32)
    last = width - 1
    dma = pltpu.SemaphoreType.DMA

    small = (neighbours, coupling, virt_energy, pair_orbs.T, occ_energy.T)
    own, amps, basis, *small = call(
        lead_kernel,
        [tile, stack, stack] + [(VMEM, value.shape, value.dtype) for value in small],
        [(HBM, amplitudes), (HBM, bases)] + [(HBM, value) for value in small],
        2 * cube, [dma((3, max(width, len(small))))],
    )
    neighbours, coupling, virt_energy, orbs, occ = small
    own = [own] + list(call(
        rest_kernel, [tile] * last, [(SMEM, pair_count), (VMEM, amps), (VMEM, basis)],
        2 * last * cube,
    ))
    weights = tile_weights(neighbours, coupling, width, virt)

    swap = [(i, i ^ 1) for i in range(count)]
    ring = [(i, (i + 2) % count if i % 2 == 0 else (i - 2) % count) for i in range(count)]
    path = list(range(0, count, 2)) + list(range(count - 1, 0, -2))
    cycle = list(zip(path, path[1:] + path[:1]))
    half = width // 2
    near = [lax.ppermute(t, "grp", swap) for t in own]
    far = [lax.ppermute(t, "grp", ring if n in (0, 2) else cycle) for n, t in enumerate(near)]
    token = neighbours
    for _ in range(width):
        mark = [(VMEM, token.shape, token.dtype)]
        token = call(mark_kernel, mark, [(VMEM, token)], 1)[0]

    pieces = row_pieces(integrals)
    aux = sum(piece.shape[1] for piece in pieces)
    base = call(
        integ_kernel, [wide],
        [(SMEM, orbs), (SMEM, occ), (SMEM, pair_count), (VMEM, virt_energy), (HBM, amplitudes)]
        + [(VMEM, piece) for piece in pieces], 2 * width * virt * virt * aux,
        [VMEM((width, virt, virt), BF16), dma((width,))],
    )[0]
    place = list(range(width)) + list(range(2 * width, 2 * width + half))
    sums = call(
        functools.partial(gather_kernel, place), [wide],
        [(SMEM, pair_count), (VMEM, weights)] + [(HBM, t) for t in own]
        + [(VMEM, t) for t in near + far[:half]],
        8 * width * virt * virt, [VMEM((width, virt, virt), BF16), dma((width,))],
    )[0]
    return call(
        functools.partial(final_kernel, range(2 * width + half, 3 * width)),
        [(pl.ANY, (width, virt, virt), F32)],
        [(SMEM, pair_count), (VMEM, token), (VMEM, weights), (VMEM, base), (VMEM, bases), (VMEM, sums)]
        + [(VMEM, t) for t in far[half:]],
        2 * width * cube, [VMEM((width, virt, virt), F32), dma((width,))],
    )[0]


def solution(mesh):
    placed = (
        P("grp", "row", None),
        P("grp", "row", None),
        P("grp", "row"),
        P("grp", "row"),
        P("grp", "row"),
        P("grp", "row"),
        P("grp", "row", None),
        P("grp", "row"),
        P("grp", "row"),
    )

    return jax.shard_map(
        local, mesh=mesh, in_specs=placed, out_specs=P("grp", "row", None), check_vma=False
    )
```

```python
import functools

import jax
import jax.numpy as jnp
from jax import lax
from jax.experimental import pallas as pl
from jax.experimental.pallas import tpu as pltpu
from jax.sharding import PartitionSpec as P


BF16 = jnp.bfloat16
F32 = jnp.float32
VMEM = pltpu.VMEM
SMEM = pltpu.SMEM
HBM = pltpu.HBM
GRANT = 8 << 20


def dot(a, b, dims):
    return lax.dot_general(a, b, (dims, ((), ())), preferred_element_type=F32)


def call(kernel, outs, inputs, flops, scratch=(), aliases=()):
    values, specs = [], []
    for space, value in inputs:
        if space in (VMEM, HBM):
            value = pltpu.with_memory_space_constraint(value, space)
        values.append(value)
        specs.append(pl.BlockSpec(memory_space=space))
    shapes, out_specs = [], []
    for space, shape, dtype in outs:
        plain = space is pl.ANY
        shapes.append(jax.ShapeDtypeStruct(shape, dtype) if plain else space(shape, dtype))
        out_specs.append(pl.BlockSpec(memory_space=space))
    size = sum(value.size * value.dtype.itemsize for value in values)
    return pl.pallas_call(
        kernel,
        out_shape=shapes,
        in_specs=specs,
        out_specs=out_specs,
        scratch_shapes=scratch,
        input_output_aliases=dict(aliases),
        cost_estimate=pl.CostEstimate(flops=flops, bytes_accessed=16 * size, transcendentals=0),
        compiler_params=pltpu.CompilerParams(vmem_limit_bytes=GRANT),
    )(*values)


def transform(base, amp):
    first = dot(base, amp, ((1,), (0,))).astype(BF16)
    return dot(first, base, ((1,), (1,))).astype(BF16)


def lead_kernel(amps, bases, *refs):
    small = (len(refs) - 4) // 2
    sources, (out, amps_out, bases_out) = refs[:small], refs[small : small + 3]
    targets, sems = refs[small + 3 : -1], refs[-1]
    width = amps.shape[0]
    loads = [
        [
            pltpu.make_async_copy(bases.at[slot], bases_out.at[slot], sems.at[0, slot]),
            pltpu.make_async_copy(amps.at[slot], amps_out.at[slot], sems.at[1, slot]),
        ]
        for slot in range(width)
    ]
    others = [
        pltpu.make_async_copy(source, target, sems.at[2, n])
        for n, (source, target) in enumerate(zip(sources, targets))
    ]
    for load in sum(loads, []) + others:
        load.start()
    for load in loads[0]:
        load.wait()
    out[...] = transform(bases_out[0], amps_out[0])
    for load in sum(loads[1:], []) + others:
        load.wait()


def rest_kernel(count, amps, bases, *outs):
    for slot, out in enumerate(outs, 1):
        amp = jnp.where(slot < count[0, 0], amps[slot], jnp.zeros((), BF16))
        out[...] = transform(bases[slot], amp)


def mark_kernel(source, out):
    out[...] = source[...]


def in_halves(count, width, work):
    half = width // 2
    work(range(half))

    @pl.when(count[0, 0] > half)
    def _():
        work(range(half, width))


def integ_kernel(orbs, occ, count, energy, amps, *refs):
    pieces, (out, held, sems) = refs[:-3], refs[-3:]
    width = amps.shape[0]
    loads = [pltpu.make_async_copy(amps.at[s], held.at[s], sems.at[s]) for s in range(width)]
    for load in loads:
        load.start()
    column = energy[...].T
    left = [piece[orbs[0, 0]].T for piece in pieces]

    def products(slots):
        for slot in slots:
            terms = [dot(a, b[orbs[1, slot]], ((1,), (0,))) for a, b in zip(left, pieces)]
            out[slot] = sum(terms[1:], terms[0])

    def energies(slots):
        for slot in slots:
            denom = column[:, slot : slot + 1] + energy[slot : slot + 1, :] - occ[0, slot]
            out[slot] += denom * held[slot].astype(F32)

    in_halves(count, width, products)
    for load in loads:
        load.wait()
    in_halves(count, width, energies)


def add_tiles(rows, columns, weights, tiles, out, slots, before):
    total = weights.shape[0] // out.shape[0]

    def step(block, carry):
        at = pl.ds(pl.multiple_of(block * rows, rows), rows)
        values = [tile[at, :].astype(F32) for tile in tiles]
        for slot in slots:
            acc = out[slot, at, :] if before else None
            for m, value in zip(columns, values):
                row = slot * total + m
                term = weights[row : row + 1, :] * value
                acc = term if acc is None else acc + term
            out[slot, at, :] = acc
        return carry

    lax.fori_loop(0, out.shape[1] // rows, step, 0)


def gather_kernel(columns, count, weights, *refs):
    tiles, (out, held, sems) = refs[:-3], refs[-3:]
    width = out.shape[0]
    own, tiles = tiles[:width], tiles[width:]
    loads = [pltpu.make_async_copy(own[s], held.at[s], sems.at[s]) for s in range(width)]
    for load in loads:
        load.start()
    in_halves(count, width, lambda slots: add_tiles(16, columns, weights, tiles, out, slots, False))
    for load in loads:
        load.wait()
    own = [held.at[s] for s in range(width)]
    place = range(width, 2 * width)
    in_halves(count, width, lambda slots: add_tiles(16, place, weights, own, out, slots, True))


def final_kernel(columns, count, token, weights, base, bases, sums, *refs):
    tiles, (out, held, sems) = refs[:-3], refs[-3:]
    width = base.shape[0]
    half = width // 2
    total = weights.shape[0] // width
    stores = [pltpu.make_async_copy(held.at[s], out.at[s], sems.at[s]) for s in range(width)]

    @pl.when(count[0, 0] <= half)
    def _():
        for slot in range(half, width):
            held[slot] = jnp.zeros(held.shape[1:], F32)
            stores[slot].start()

    def some(slots):
        combined = []
        for slot in slots:
            acc = sums[slot]
            for m, tile in zip(columns, tiles):
                row = slot * total + m
                acc = acc + weights[row : row + 1, :] * tile[...].astype(F32)
            combined.append(acc.astype(BF16))
        firsts = [dot(bases[s], c, ((0,), (0,))).astype(BF16) for s, c in zip(slots, combined)]
        for slot, first in zip(slots, firsts):
            back = dot(first, bases[slot], ((1,), (0,)))
            value = base[slot] - back
            held[slot] = jnp.where(slot < count[0, 0], value, jnp.float32(0))
            stores[slot].start()

    in_halves(count, width, some)
    for store in stores:
        store.wait()


def row_pieces(array):
    count = lax.axis_size("row")
    pieces = [array]
    if count & (count - 1):
        for shift in range(1, count):
            pairs = [(i, (i + shift) % count) for i in range(count)]
            pieces.append(lax.ppermute(array, "row", pairs))
        return pieces
    step = count // 2
    while step:
        pairs = [(i, i ^ step) for i in range(count)]
        piece = jnp.concatenate(pieces, axis=1)
        pieces = [piece, lax.ppermute(piece, "row", pairs)]
        step //= 2
    return pieces


def whole_pairs(pairs):
    rows, count = lax.axis_size("row"), lax.axis_size("grp")
    return [(r * count + i, (r ^ 1 if i == j else r) * count + j) for r in range(rows) for i, j in pairs]


def tile_weights(neighbours, coupling, width, virt):
    levels = lax.axis_size("grp") // 2
    group = lax.axis_index("grp")
    level = lax.shift_right_logical(group, 1)
    even = (group & 1) == 0
    inside = jnp.where(even, level > 0, level < levels - 1)
    block = (neighbours >= width).astype(jnp.int32) + (neighbours >= 2 * width).astype(jnp.int32)
    kind = jnp.where(even, 2 - block, block)
    scale = jnp.where((kind < 2) | inside, coupling, 0.0)
    place = neighbours + (kind - block) * width
    shape = (width, 3 * width, virt, neighbours.shape[1])
    index = lax.broadcasted_iota(jnp.int32, shape, 1)
    hit = place[:, None, None, :] == index
    table = jnp.sum(jnp.where(hit, scale[:, None, None, :], 0.0), axis=3)
    return table.reshape(width * 3 * width, virt)


def local(
    integrals,
    amplitudes,
    pair_orbs,
    pair_count,
    neighbours,
    coupling,
    bases,
    virt_energy,
    occ_energy,
):
    width, virt = amplitudes.shape[0], amplitudes.shape[1]
    count = lax.axis_size("grp")
    cube = 2 * virt * virt * virt
    tile = (VMEM, (virt, virt), BF16)
    stack = (VMEM, (width, virt, virt), BF16)
    wide = (VMEM, (width, virt, virt), F32)
    last = width - 1
    dma = pltpu.SemaphoreType.DMA

    small = (neighbours, coupling, virt_energy, pair_orbs.T, occ_energy.T)
    own, amps, basis, *small = call(
        lead_kernel,
        [tile, stack, stack] + [(VMEM, value.shape, value.dtype) for value in small],
        [(HBM, amplitudes), (HBM, bases)] + [(HBM, value) for value in small],
        2 * cube, [dma((3, max(width, len(small))))],
    )
    neighbours, coupling, virt_energy, orbs, occ = small
    own = [own] + list(call(
        rest_kernel, [tile] * last, [(SMEM, pair_count), (VMEM, amps), (VMEM, basis)],
        2 * last * cube,
    ))
    weights = tile_weights(neighbours, coupling, width, virt)

    swap = [(i, i ^ 1) for i in range(count)]
    ring = [(i, (i + 2) % count if i % 2 == 0 else (i - 2) % count) for i in range(count)]
    path = list(range(0, count, 2)) + list(range(count - 1, 0, -2))
    cycle = list(zip(path, path[1:] + path[:1]))
    direct = [(i, i - 1 if i % 2 == 0 else i + 1) for i in range(1, count - 1)]
    direct = whole_pairs(direct + [(0, 0), (count - 1, count - 1)])
    half = width // 2
    near = [lax.ppermute(t, "grp", swap) for t in own]
    far = [lax.ppermute(t, "grp", ring if n < half else cycle) for n, t in enumerate(near[:last])]
    far.append(lax.ppermute(own[last], ("row", "grp"), direct))
    token = neighbours
    for _ in range(width):
        mark = [(VMEM, token.shape, token.dtype)]
        token = call(mark_kernel, mark, [(VMEM, token)], 1)[0]

    pieces = row_pieces(integrals)
    aux = sum(piece.shape[1] for piece in pieces)
    base = call(
        integ_kernel, [wide],
        [(SMEM, orbs), (SMEM, occ), (SMEM, pair_count), (VMEM, virt_energy), (HBM, amplitudes)]
        + [(VMEM, piece) for piece in pieces], 2 * width * virt * virt * aux,
        [VMEM((width, virt, virt), BF16), dma((width,))],
    )[0]
    place = list(range(width)) + list(range(2 * width, 2 * width + half))
    sums = call(
        functools.partial(gather_kernel, place), [wide],
        [(SMEM, pair_count), (VMEM, weights)] + [(HBM, t) for t in own]
        + [(VMEM, t) for t in near + far[:half]],
        8 * width * virt * virt, [VMEM((width, virt, virt), BF16), dma((width,))],
    )[0]
    return call(
        functools.partial(final_kernel, range(2 * width + half, 3 * width)),
        [(pl.ANY, (width, virt, virt), F32)],
        [(SMEM, pair_count), (VMEM, token), (VMEM, weights), (VMEM, base), (VMEM, bases), (VMEM, sums)]
        + [(VMEM, t) for t in far[half:]],
        2 * width * cube, [VMEM((width, virt, virt), F32), dma((width,))],
    )[0]


def solution(mesh):
    placed = (
        P("grp", "row", None),
        P("grp", "row", None),
        P("grp", "row"),
        P("grp", "row"),
        P("grp", "row"),
        P("grp", "row"),
        P("grp", "row", None),
        P("grp", "row"),
        P("grp", "row"),
    )

    return jax.shard_map(
        local, mesh=mesh, in_specs=placed, out_specs=P("grp", "row", None), check_vma=False
    )
```

```python
import functools

import jax
import jax.numpy as jnp
from jax import lax
from jax.experimental import pallas as pl
from jax.experimental.pallas import tpu as pltpu
from jax.sharding import PartitionSpec as P


BF16 = jnp.bfloat16
F32 = jnp.float32
VMEM = pltpu.VMEM
SMEM = pltpu.SMEM
HBM = pltpu.HBM
GRANT = 8 << 20


def dot(a, b, dims):
    return lax.dot_general(a, b, (dims, ((), ())), preferred_element_type=F32)


def call(kernel, outs, inputs, flops, scratch=(), aliases=()):
    values, specs = [], []
    for space, value in inputs:
        if space in (VMEM, HBM):
            value = pltpu.with_memory_space_constraint(value, space)
        values.append(value)
        specs.append(pl.BlockSpec(memory_space=space))
    shapes, out_specs = [], []
    for space, shape, dtype in outs:
        plain = space is pl.ANY
        shapes.append(jax.ShapeDtypeStruct(shape, dtype) if plain else space(shape, dtype))
        out_specs.append(pl.BlockSpec(memory_space=space))
    size = sum(value.size * value.dtype.itemsize for value in values)
    return pl.pallas_call(
        kernel,
        out_shape=shapes,
        in_specs=specs,
        out_specs=out_specs,
        scratch_shapes=scratch,
        input_output_aliases=dict(aliases),
        cost_estimate=pl.CostEstimate(flops=flops, bytes_accessed=16 * size, transcendentals=0),
        compiler_params=pltpu.CompilerParams(vmem_limit_bytes=GRANT),
    )(*values)


def transform(base, amp):
    first = dot(base, amp, ((1,), (0,))).astype(BF16)
    return dot(first, base, ((1,), (1,))).astype(BF16)


def lead_kernel(amps, bases, *refs):
    small = (len(refs) - 4) // 2
    sources, (out, amps_out, bases_out) = refs[:small], refs[small : small + 3]
    targets, sems = refs[small + 3 : -1], refs[-1]
    width = amps.shape[0]
    loads = [
        [
            pltpu.make_async_copy(bases.at[slot], bases_out.at[slot], sems.at[0, slot]),
            pltpu.make_async_copy(amps.at[slot], amps_out.at[slot], sems.at[1, slot]),
        ]
        for slot in range(width)
    ]
    others = [
        pltpu.make_async_copy(source, target, sems.at[2, n])
        for n, (source, target) in enumerate(zip(sources, targets))
    ]
    for load in sum(loads, []) + others:
        load.start()
    for load in loads[0]:
        load.wait()
    out[...] = transform(bases_out[0], amps_out[0])
    for load in sum(loads[1:], []) + others:
        load.wait()


def rest_kernel(count, amps, bases, *outs):
    for slot, out in enumerate(outs, 1):
        amp = jnp.where(slot < count[0, 0], amps[slot], jnp.zeros((), BF16))
        out[...] = transform(bases[slot], amp)


def mark_kernel(source, out):
    out[...] = source[...]


def in_halves(count, width, work):
    half = width // 2
    work(range(half))

    @pl.when(count[0, 0] > half)
    def _():
        work(range(half, width))


def integ_kernel(orbs, occ, count, energy, amps, *refs):
    pieces, (out, held, sems) = refs[:-3], refs[-3:]
    width = amps.shape[0]
    loads = [pltpu.make_async_copy(amps.at[s], held.at[s], sems.at[s]) for s in range(width)]
    for load in loads:
        load.start()
    column = energy[...].T
    left = [piece[orbs[0, 0]].T for piece in pieces]

    def products(slots):
        for slot in slots:
            terms = [dot(a, b[orbs[1, slot]], ((1,), (0,))) for a, b in zip(left, pieces)]
            out[slot] = sum(terms[1:], terms[0])

    def energies(slots):
        for slot in slots:
            denom = column[:, slot : slot + 1] + energy[slot : slot + 1, :] - occ[0, slot]
            out[slot] += denom * held[slot].astype(F32)

    in_halves(count, width, products)
    for load in loads:
        load.wait()
    in_halves(count, width, energies)


def add_tiles(rows, columns, weights, tiles, out, slots, before):
    total = weights.shape[0] // out.shape[0]

    def step(block, carry):
        at = pl.ds(pl.multiple_of(block * rows, rows), rows)
        values = [tile[at, :].astype(F32) for tile in tiles]
        for slot in slots:
            acc = out[slot, at, :] if before else None
            for m, value in zip(columns, values):
                row = slot * total + m
                term = weights[row : row + 1, :] * value
                acc = term if acc is None else acc + term
            out[slot, at, :] = acc
        return carry

    lax.fori_loop(0, out.shape[1] // rows, step, 0)


def gather_kernel(columns, count, weights, *refs):
    tiles, (out, held, sems) = refs[:-3], refs[-3:]
    width = out.shape[0]
    own, tiles = tiles[:width], tiles[width:]
    loads = [pltpu.make_async_copy(own[s], held.at[s], sems.at[s]) for s in range(width)]
    for load in loads:
        load.start()
    in_halves(count, width, lambda slots: add_tiles(16, columns, weights, tiles, out, slots, False))
    for load in loads:
        load.wait()
    own = [held.at[s] for s in range(width)]
    place = range(width, 2 * width)
    in_halves(count, width, lambda slots: add_tiles(16, place, weights, own, out, slots, True))


def final_kernel(columns, count, token, weights, base, bases, sums, *refs):
    tiles, (out, held, sems) = refs[:-3], refs[-3:]
    width = base.shape[0]
    half = width // 2
    total = weights.shape[0] // width
    parts = sems.shape[1]
    height = base.shape[1] // parts
    stores = []
    for slot in range(width):
        cuts = [(slot, pl.ds(part * height, height)) for part in range(parts)]
        stores.append([
            pltpu.make_async_copy(held.at[cut], out.at[cut], sems.at[slot, part])
            for part, cut in enumerate(cuts)
        ])

    @pl.when(count[0, 0] <= half)
    def _():
        for slot in range(half, width):
            held[slot] = jnp.zeros(held.shape[1:], F32)
            for store in stores[slot]:
                store.start()

    def some(slots):
        combined = []
        for slot in slots:
            acc = sums[slot]
            for m, tile in zip(columns, tiles):
                row = slot * total + m
                acc = acc + weights[row : row + 1, :] * tile[...].astype(F32)
            combined.append(acc.astype(BF16))
        firsts = [dot(bases[s], c, ((0,), (0,))).astype(BF16) for s, c in zip(slots, combined)]
        for slot, first in zip(slots, firsts):
            for part in range(parts):
                rows = pl.ds(part * height, height)
                piece = first[part * height : (part + 1) * height]
                value = base[slot, rows] - dot(piece, bases[slot], ((1,), (0,)))
                held[slot, rows] = jnp.where(slot < count[0, 0], value, jnp.float32(0))
                stores[slot][part].start()

    in_halves(count, width, some)
    for store in sum(stores, []):
        store.wait()


def row_pieces(array):
    count = lax.axis_size("row")
    pieces = [array]
    if count & (count - 1):
        for shift in range(1, count):
            pairs = [(i, (i + shift) % count) for i in range(count)]
            pieces.append(lax.ppermute(array, "row", pairs))
        return pieces
    step = count // 2
    while step:
        pairs = [(i, i ^ step) for i in range(count)]
        piece = jnp.concatenate(pieces, axis=1)
        pieces = [piece, lax.ppermute(piece, "row", pairs)]
        step //= 2
    return pieces


def whole_pairs(pairs):
    rows, count = lax.axis_size("row"), lax.axis_size("grp")
    return [(r * count + i, (r ^ 1 if i == j else r) * count + j) for r in range(rows) for i, j in pairs]


def tile_weights(neighbours, coupling, width, virt):
    levels = lax.axis_size("grp") // 2
    group = lax.axis_index("grp")
    level = lax.shift_right_logical(group, 1)
    even = (group & 1) == 0
    inside = jnp.where(even, level > 0, level < levels - 1)
    block = (neighbours >= width).astype(jnp.int32) + (neighbours >= 2 * width).astype(jnp.int32)
    kind = jnp.where(even, 2 - block, block)
    scale = jnp.where((kind < 2) | inside, coupling, 0.0)
    place = neighbours + (kind - block) * width
    shape = (width, 3 * width, virt, neighbours.shape[1])
    index = lax.broadcasted_iota(jnp.int32, shape, 1)
    hit = place[:, None, None, :] == index
    table = jnp.sum(jnp.where(hit, scale[:, None, None, :], 0.0), axis=3)
    return table.reshape(width * 3 * width, virt)


def local(
    integrals,
    amplitudes,
    pair_orbs,
    pair_count,
    neighbours,
    coupling,
    bases,
    virt_energy,
    occ_energy,
):
    width, virt = amplitudes.shape[0], amplitudes.shape[1]
    count = lax.axis_size("grp")
    cube = 2 * virt * virt * virt
    tile = (VMEM, (virt, virt), BF16)
    stack = (VMEM, (width, virt, virt), BF16)
    wide = (VMEM, (width, virt, virt), F32)
    last = width - 1
    dma = pltpu.SemaphoreType.DMA

    small = (neighbours, coupling, virt_energy, pair_orbs.T, occ_energy.T)
    own, amps, basis, *small = call(
        lead_kernel,
        [tile, stack, stack] + [(VMEM, value.shape, value.dtype) for value in small],
        [(HBM, amplitudes), (HBM, bases)] + [(HBM, value) for value in small],
        2 * cube, [dma((3, max(width, len(small))))],
    )
    neighbours, coupling, virt_energy, orbs, occ = small
    own = [own] + list(call(
        rest_kernel, [tile] * last, [(SMEM, pair_count), (VMEM, amps), (VMEM, basis)],
        2 * last * cube,
    ))
    weights = tile_weights(neighbours, coupling, width, virt)

    swap = [(i, i ^ 1) for i in range(count)]
    ring = [(i, (i + 2) % count if i % 2 == 0 else (i - 2) % count) for i in range(count)]
    path = list(range(0, count, 2)) + list(range(count - 1, 0, -2))
    cycle = list(zip(path, path[1:] + path[:1]))
    direct = [(i, i - 1 if i % 2 == 0 else i + 1) for i in range(1, count - 1)]
    direct = whole_pairs(direct + [(0, 0), (count - 1, count - 1)])
    half = width // 2
    near = [lax.ppermute(t, "grp", swap) for t in own]
    far = [lax.ppermute(t, "grp", ring if n < half else cycle) for n, t in enumerate(near[:last])]
    far.append(lax.ppermute(own[last], ("row", "grp"), direct))
    token = neighbours
    for _ in range(width):
        mark = [(VMEM, token.shape, token.dtype)]
        token = call(mark_kernel, mark, [(VMEM, token)], 1)[0]

    pieces = row_pieces(integrals)
    aux = sum(piece.shape[1] for piece in pieces)
    base = call(
        integ_kernel, [wide],
        [(SMEM, orbs), (SMEM, occ), (SMEM, pair_count), (VMEM, virt_energy), (HBM, amplitudes)]
        + [(VMEM, piece) for piece in pieces], 2 * width * virt * virt * aux,
        [VMEM((width, virt, virt), BF16), dma((width,))],
    )[0]
    place = list(range(width)) + list(range(2 * width, 2 * width + half))
    sums = call(
        functools.partial(gather_kernel, place), [wide],
        [(SMEM, pair_count), (VMEM, weights)] + [(HBM, t) for t in own]
        + [(VMEM, t) for t in near + far[:half]],
        8 * width * virt * virt, [VMEM((width, virt, virt), BF16), dma((width,))],
    )[0]
    return call(
        functools.partial(final_kernel, range(2 * width + half, 3 * width)),
        [(pl.ANY, (width, virt, virt), F32)],
        [(SMEM, pair_count), (VMEM, token), (VMEM, weights), (VMEM, base), (VMEM, bases), (VMEM, sums)]
        + [(VMEM, t) for t in far[half:]],
        2 * width * cube, [VMEM((width, virt, virt), F32), dma((width, 2))],
    )[0]


def solution(mesh):
    placed = (
        P("grp", "row", None),
        P("grp", "row", None),
        P("grp", "row"),
        P("grp", "row"),
        P("grp", "row"),
        P("grp", "row"),
        P("grp", "row", None),
        P("grp", "row"),
        P("grp", "row"),
    )

    return jax.shard_map(
        local, mesh=mesh, in_specs=placed, out_specs=P("grp", "row", None), check_vma=False
    )
```
